32 devices in a mesh: fsdp: 2 (over y), ctx: 4 (over x, core), tp: 4 (over z).
Axes of the slice: x: 2, y: 2, z: 4, core: 2. Of those that a mesh axis runs over, the one named last changes fastest.
Arguments:
- tokens: bfloat16 [2048, 2048], P(('fsdp', 'ctx')), may hold values from -6 to 6
- doc_ids: int32 [2048], P('fsdp'), may hold values from 0 to 3, as said below
- positions: int32 [2048], P(('fsdp', 'ctx')), may hold values from 0 to 1022, as said below
- attn_gain: bfloat16 [2, 2048], P(None, ('fsdp', 'ctx')), may hold values from 0.099609375 to 1.8984375
- q_weight: bfloat16 [2, 2048, 2048], P(None, ('fsdp', 'ctx'), 'tp'), may hold values from -0.125 to 0.125
- k_weight: bfloat16 [2, 2048, 512], P(None, ('fsdp', 'ctx'), 'tp'), may hold values from -0.125 to 0.125
- v_weight: bfloat16 [2, 2048, 512], P(None, ('fsdp', 'ctx'), 'tp'), may hold values from -0.125 to 0.125
- o_weight: bfloat16 [2, 2048, 2048], P(None, ('fsdp', 'ctx'), 'tp'), may hold values from -0.5 to 0.5
- mlp_gain: bfloat16 [2, 2048], P(None, ('fsdp', 'ctx')), may hold values from 0.099609375 to 1.8984375
- gate_weight: bfloat16 [2, 2048, 8192], P(None, ('fsdp', 'ctx'), 'tp'), may hold values from -0.125 to 0.125
- up_weight: bfloat16 [2, 2048, 8192], P(None, ('fsdp', 'ctx'), 'tp'), may hold values from -0.125 to 0.125
- down_weight: bfloat16 [2, 2048, 8192], P(None, ('fsdp', 'ctx'), 'tp'), may hold values from -0.0625 to 0.0625
- out_grad: bfloat16 [2048, 2048], P(('fsdp', 'ctx')), may hold values from -6 to 6
Outputs:
- output: bfloat16 [2048, 2048], P(('fsdp', 'ctx'))
- tokens_grad: float32 [2048, 2048], P(('fsdp', 'ctx'))
- attn_gain_grad: float32 [2, 2048], P(None, ('fsdp', 'ctx'))
- q_grad: float32 [2, 2048, 2048], P(None, ('fsdp', 'ctx'), 'tp')
- k_grad: float32 [2, 2048, 512], P(None, ('fsdp', 'ctx'), 'tp')
- v_grad: float32 [2, 2048, 512], P(None, ('fsdp', 'ctx'), 'tp')
- o_grad: float32 [2, 2048, 2048], P(None, ('fsdp', 'ctx'), 'tp')
- mlp_gain_grad: float32 [2, 2048], P(None, ('fsdp', 'ctx'))
- gate_grad: float32 [2, 2048, 8192], P(None, ('fsdp', 'ctx'), 'tp')
- up_grad: float32 [2, 2048, 8192], P(None, ('fsdp', 'ctx'), 'tp')
- down_grad: float32 [2, 2048, 8192], P(None, ('fsdp', 'ctx'), 'tp')
The draws below stay inside these ranges and needn't reach their ends.
Inputs may be any that keep to these rules, and one draw needn't show every extreme that they name: `doc_ids`: within each sequence of 1024 tokens the numbers never fall, start at 0 and end at 3; a number may be absent. `positions`: each token's position is its index in its sequence minus that of the first token of its document; a document holds at most 1023 tokens.
All inputs are finite; a program needn't handle non-finite values.
Results may differ from the reference program's by a relative error of at most 0.035.
Values may be sent and summed in bfloat16 or wider, within the bound.
No kernel may reach another device: no remote copies, remote signals or barrier semaphores. Data moves between devices by JAX's collectives and lax.ppermute only.
A program may use at most 256 MiB of HBM per device.

```python
import math
import jax
import jax.numpy as jnp
from jax import lax

D = 2048
HEADS = 32
KV_HEADS = 8
HEAD_DIM = 64
FF = 8192
LAYERS = 2
CUTS = 3
LENGTH = 1024
TOKENS = 2048


def document_cuts(key):
    drawn = jax.random.randint(jax.random.fold_in(key, 17), (TOKENS // LENGTH, CUTS), 1, LENGTH)
    first_row = jnp.arange(TOKENS // LENGTH, dtype=jnp.int32)[:, None] == 0
    return jnp.where(first_row, jnp.int32(LENGTH - 1), drawn)


def draw_doc_ids(key, part):
    cut_points = document_cuts(key)
    index_row = jnp.arange(LENGTH, dtype=jnp.int32)
    passed = index_row[None, :, None] >= cut_points[:, None, :]
    return jnp.sum(passed.astype(jnp.int32), axis=2).reshape(TOKENS)


def draw_positions(key, part):
    cut_points = document_cuts(key)
    index_row = jnp.arange(LENGTH, dtype=jnp.int32)
    passed = index_row[None, :, None] >= cut_points[:, None, :]
    begins = jnp.max(jnp.where(passed, cut_points[:, None, :], 0), axis=2)
    return (index_row[None, :] - begins).reshape(TOKENS)


def raised(values, key, source, target, shards_of, factor):
    owner, partner = [(jnp.arange(values.shape[position]) // (values.shape[position] // shards_of)).reshape([-1 if axis == position else 1 for axis in range(values.ndim)]) for position in (source, target)]
    chosen = jax.random.permutation(key, shards_of)[partner]
    strong = (owner == chosen) | (owner == (partner + shards_of // 2) % shards_of)
    return jnp.where(strong, factor * values, values)


def level_of(own_key, shape, shards, smallest, top_value):
    loudness, own = 1.0, jax.random.fold_in(own_key, 6)
    for dim, blocks in shards:
        draws = jnp.exp(jax.random.uniform(jax.random.fold_in(own, dim), (blocks,), jnp.float32, smallest / len(shards), top_value / len(shards)))
        loudness = loudness * jnp.repeat(draws, shape[dim] // blocks).reshape([-1 if axis == dim else 1 for axis in range(len(shape))])
    return loudness


def normal_values(rng, extent, deviation, reach, shards=(), held_as=jnp.bfloat16):
    values = deviation * jax.random.normal(rng, extent, jnp.float32)
    if shards:
        values = values * level_of(rng, extent, shards, -0.22, 0.18)
    return jnp.clip(values, -reach, reach).astype(held_as)


def noise_with(stream_key, shape, spread, reach, pieces, heavy, held_as=jnp.bfloat16):
    values = spread * jax.random.normal(stream_key, shape, jnp.float32)
    if pieces:
        values = values * level_of(stream_key, shape, pieces, -0.22, 0.18)
    return jnp.clip(raised(values, jax.random.fold_in(stream_key, 3), *heavy), -reach, reach).astype(held_as)


def setup_inputs(seed: int = 0) -> dict:
    splits = jax.random.split(jax.random.key(seed), 14)
    tokens = noise_with(splits[0], (TOKENS, D), 1.0, 6.0, ((0, 8),), (0, 1, 8, 2.0))
    doc_ids = draw_doc_ids(jax.random.fold_in(splits[13], 71), 0)
    positions = draw_positions(jax.random.fold_in(splits[13], 71), 0)
    attn_gain = jnp.clip(1.0 + 0.18 * jax.random.normal(splits[3], (LAYERS, D), jnp.float32), 0.099609375, 1.8984375).astype(jnp.bfloat16)
    q_weight = normal_values(splits[4], (LAYERS, D, HEADS * HEAD_DIM), D ** -0.5, 0.125, ((1, 8), (2, 4)))
    k_weight = normal_values(splits[5], (LAYERS, D, KV_HEADS * HEAD_DIM), D ** -0.5, 0.125, ((1, 8), (2, 4)))
    v_weight = normal_values(splits[6], (LAYERS, D, KV_HEADS * HEAD_DIM), D ** -0.5, 0.125, ((1, 8), (2, 4)))
    o_weight = normal_values(splits[7], (LAYERS, D, HEADS * HEAD_DIM), (HEADS * HEAD_DIM // 16) ** -0.5, 0.5, ((1, 8), (2, 4)))
    mlp_gain = jnp.clip(1.0 + 0.18 * jax.random.normal(splits[8], (LAYERS, D), jnp.float32), 0.099609375, 1.8984375).astype(jnp.bfloat16)
    gate_weight = normal_values(splits[9], (LAYERS, D, FF), D ** -0.5, 0.125, ((1, 8), (2, 4)))
    up_weight = normal_values(splits[10], (LAYERS, D, FF), D ** -0.5, 0.125, ((1, 8), (2, 4)))
    down_weight = normal_values(splits[11], (LAYERS, D, FF), FF ** -0.5, 0.0625, ((1, 8), (2, 4)))
    out_grad = noise_with(splits[12], (TOKENS, D), 1.0, 6.0, ((0, 8),), (0, 1, 8, 2.0))
    return {"tokens": tokens, "doc_ids": doc_ids, "positions": positions, "attn_gain": attn_gain, "q_weight": q_weight, "k_weight": k_weight, "v_weight": v_weight, "o_weight": o_weight, "mlp_gain": mlp_gain, "gate_weight": gate_weight, "up_weight": up_weight, "down_weight": down_weight, "out_grad": out_grad}


ROPE_BASE = 500000.0
EPSILON = 1e-05
NEGATIVE = -1e+30
PRECISE = lax.Precision.HIGHEST

@jax.custom_vjp
def low(v):
    return lax.optimization_barrier(v.astype(jnp.bfloat16)).astype(jnp.float32)

@jax.custom_vjp
def low_back(v):
    return v

def low_keep(v):
    return (low(v), None)

def low_pass(kept, grad):
    return (grad,)

def back_keep(v):
    return (v, None)

def back_low(kept, grad):
    return (low(grad),)
low.defvjp(low_keep, low_pass)
low_back.defvjp(back_keep, back_low)

def tables(position_row):
    half_dim = HEAD_DIM // 2
    inverse = jnp.exp(jnp.arange(half_dim, dtype=jnp.float32) * (-2.0 * math.log(ROPE_BASE) / HEAD_DIM))
    angles = position_row.astype(jnp.float32)[:, None] * inverse[None, :]
    return (jnp.cos(angles)[:, None, :], jnp.sin(angles)[:, None, :])

def rotate(vector, cosine, sine_part):
    half_dim = vector.shape[-1] // 2
    first_half = vector[..., :half_dim]
    second = vector[..., half_dim:]
    return jnp.concatenate([first_half * cosine - second * sine_part, second * cosine + first_half * sine_part], axis=-1)

def normed(values_in):
    return values_in * lax.rsqrt(lax.optimization_barrier(jnp.mean(values_in * values_in, axis=-1, keepdims=True)) + EPSILON)

def matmul(left_side, right_side):
    return jnp.dot(left_side, right_side, precision=PRECISE, preferred_element_type=jnp.float32)

def attend(queries, keys_rot, values_low, doc_row):
    length = queries.shape[0]
    block_rows = min(512, length)
    group_size = HEADS // KV_HEADS
    scaling = 1.0 / math.sqrt(HEAD_DIM)
    grouped = queries.reshape(length // block_rows, block_rows, KV_HEADS, group_size, HEAD_DIM)
    block_starts = jnp.arange(length // block_rows, dtype=jnp.int32) * block_rows
    key_index = jnp.arange(length, dtype=jnp.int32)

    @jax.checkpoint
    def one_block(block_item):
        query_block, row_start = block_item
        raw_score = jnp.einsum('qgrd,kgd->grqk', query_block, keys_rot, precision=PRECISE)
        scores = low_back(scaling * raw_score)
        row_index = row_start + jnp.arange(block_rows, dtype=jnp.int32)
        row_doc = lax.dynamic_slice_in_dim(doc_row, row_start, block_rows)
        visible = (key_index[None, :] <= row_index[:, None]) & (doc_row[None, :] == row_doc[:, None])
        scores = jnp.where(visible[None, None], scores, NEGATIVE)
        top_row = lax.optimization_barrier(jnp.max(scores, axis=-1, keepdims=True))
        powered = jnp.exp(scores - top_row)
        shares = powered / lax.optimization_barrier(jnp.sum(powered, axis=-1, keepdims=True))
        return jnp.einsum('grqk,kgd->qgrd', low(shares), values_low, precision=PRECISE)
    attended = lax.map(one_block, (grouped, block_starts))
    return attended.reshape(length, HEADS * HEAD_DIM)

def one_layer(hidden_state, doc_row, cosine, sine_part, weight_set):
    gain_attn, q_full, k_full, v_full, o_full, gain_mlp, gate_full, up_full, down_full = weight_set
    length = hidden_state.shape[0]
    attn_in = low(normed(hidden_state) * gain_attn)
    query_proj = low_back(matmul(attn_in, q_full))
    key_proj = low_back(matmul(attn_in, k_full))
    value_proj = low_back(matmul(attn_in, v_full))
    queries = low(rotate(query_proj.reshape(length, HEADS, HEAD_DIM), cosine, sine_part))
    keys_rot = low(rotate(key_proj.reshape(length, KV_HEADS, HEAD_DIM), cosine, sine_part))
    values_low = low(value_proj.reshape(length, KV_HEADS, HEAD_DIM))
    attended = low_back(attend(queries, keys_rot, values_low, doc_row))
    hidden_mid = hidden_state + low_back(matmul(low(attended), o_full.T))
    mlp_in = low(normed(hidden_mid) * gain_mlp)
    gate_proj = low_back(matmul(mlp_in, gate_full))
    up_proj = low_back(matmul(mlp_in, up_full))
    activated = low(jax.nn.silu(gate_proj) * up_proj)
    return hidden_mid + low_back(matmul(activated, down_full.T))

def forward(tokens_in, weight_list, doc_ids, positions):
    seq_count = tokens_in.shape[0] // LENGTH

    @jax.checkpoint
    def one_sequence(seq_item):
        hidden_state, doc_row, position_row = seq_item
        cosine, sine_part = tables(position_row)
        for layer_index in range(LAYERS):
            hidden_state = one_layer(hidden_state, doc_row, cosine, sine_part, tuple((weight_one[layer_index] for weight_one in weight_list)))
        return hidden_state
    result = lax.map(one_sequence, (tokens_in.reshape(seq_count, LENGTH, D), doc_ids.reshape(seq_count, LENGTH), positions.reshape(seq_count, LENGTH)))
    return result.reshape(seq_count * LENGTH, D)

def reference(tokens, doc_ids, positions, attn_gain, q_weight, k_weight, v_weight, o_weight, mlp_gain, gate_weight, up_weight, down_weight, out_grad):
    params = tuple((array_in.astype(jnp.float32) for array_in in (attn_gain, q_weight, k_weight, v_weight, o_weight, mlp_gain, gate_weight, up_weight, down_weight)))

    def run(tokens_in, *weight_list):
        return forward(tokens_in, weight_list, doc_ids, positions)
    result, pullback = jax.vjp(run, tokens.astype(jnp.float32), *params)
    gradients = pullback(out_grad.astype(jnp.float32))
    return (result.astype(jnp.bfloat16), gradients[0], gradients[1], gradients[2], gradients[3], gradients[4], gradients[5], gradients[6], gradients[7], gradients[8], gradients[9])
```

```python
import functools
import math

import jax
import jax.numpy as jnp
from jax import lax
from jax.experimental import pallas as pl
from jax.experimental.pallas import tpu as pltpu
from jax.sharding import Mesh
from jax.sharding import PartitionSpec as P

HEAD_DIM = 64
LANES = 128
ROPE_BASE = 500000.0
EPSILON = 1e-05
NEGATIVE = -1e30


PLANE = ("fsdp", "cx")
ALL_ROWS = ("fsdp", "cx", "cc")
NEAR = [(0, 1), (1, 0), (2, 3), (3, 2)]
FAR = [(0, 3), (3, 0), (1, 2), (2, 1)]
SWAP = [(0, 1), (1, 0)]

f32 = jnp.float32
bf16 = jnp.bfloat16


def dot_nn(a, b):
    return lax.dot_general(a, b, (((1,), (0,)), ((), ())), preferred_element_type=f32)


def dot_nt(a, b):
    return lax.dot_general(a, b, (((1,), (1,)), ((), ())), preferred_element_type=f32)


def dot_tn(a, b):
    return lax.dot_general(a, b, (((0,), (0,)), ((), ())), preferred_element_type=f32)


def swap_halves(slab):
    lane = lax.broadcasted_iota(jnp.int32, slab.shape, 1)
    low = lax.rem(lane, HEAD_DIM) < HEAD_DIM // 2
    return jnp.where(low, pltpu.roll(slab, LANES - HEAD_DIM // 2, 1), pltpu.roll(slab, HEAD_DIM // 2, 1))


def rotate(slab, cosine, sine):
    return slab * cosine + swap_halves(slab) * sine


def first_lanes(shape):
    return lax.broadcasted_iota(jnp.int32, shape, 1) < HEAD_DIM


def rope_kernel(x_ref, cos_ref, sin_ref, q_ref, kv_ref):
    cosine, sine = cos_ref[...], sin_ref[...]
    slabs = q_ref.shape[1] // LANES
    for j in range(slabs):
        part = pl.ds(j * LANES, LANES)
        q_ref[:, part] = rotate(x_ref[:, part], cosine, sine).astype(bf16)
    kv = x_ref[:, pl.ds(slabs * LANES, LANES)]
    kv_ref[...] = jnp.where(first_lanes(kv.shape), rotate(kv, cosine, sine), kv).astype(bf16)


def rope_forward(x, cosine, sine):
    rows, width = x.shape
    return pl.pallas_call(
        rope_kernel,
        out_shape=(
            jax.ShapeDtypeStruct((rows, width - LANES), bf16),
            jax.ShapeDtypeStruct((rows, LANES), bf16),
        ),
        cost_estimate=pl.CostEstimate(flops=rows * width * 6, bytes_accessed=rows * width * 8, transcendentals=0),
        name="rope_forward",
    )(x, cosine, sine)


def kv_back_kernel(own_ref, got_ref, cos_ref, sin_ref, out_ref):
    total = own_ref[...] + got_ref[...].astype(f32)
    out_ref[...] = jnp.where(
        first_lanes(total.shape), rotate(total, cos_ref[...], -sin_ref[...]), total
    ).astype(bf16)


def kv_backward(own, got, cosine, sine):
    return pl.pallas_call(
        kv_back_kernel,
        out_shape=jax.ShapeDtypeStruct(own.shape, bf16),
        cost_estimate=pl.CostEstimate(flops=own.size * 6, bytes_accessed=own.size * 16, transcendentals=0),
        name="kv_backward",
    )(own, got, cosine, sine)


def spread_keys(kvo_ref, kvx_ref, keys, values):
    rows = kvo_ref.shape[0]
    for number, ref in enumerate((kvo_ref, kvx_ref)):
        both = ref[...].astype(f32)
        turned = pltpu.roll(both, HEAD_DIM, 1)
        low = first_lanes(both.shape)
        keys[pl.ds(number * rows, rows), :] = jnp.where(low, both, turned).astype(bf16)
        values[pl.ds(number * rows, rows), :] = jnp.where(low, turned, both).astype(bf16)


def mask_bias(qi_ref, qd_ref, ki_ref, kd_ref):
    seen = (ki_ref[...] <= qi_ref[...]) & (kd_ref[...] == qd_ref[...])
    return jnp.where(seen, 0.0, NEGATIVE)


def attend_kernel(scaling, q_ref, kvo_ref, kvx_ref, qi_ref, qd_ref, ki_ref, kd_ref, o_ref, lse_ref, keys, values, bias):
    @pl.when((pl.program_id(0) == 0) & (pl.program_id(1) == 0))
    def _():
        spread_keys(kvo_ref, kvx_ref, keys, values)

    @pl.when(pl.program_id(1) == 0)
    def _():
        bias[...] = mask_bias(qi_ref, qd_ref, ki_ref, kd_ref)

    pair = q_ref[...]
    low = first_lanes(pair.shape)
    outs, logs = [], []
    for parity in range(2):
        mine = low if parity == 0 else jnp.logical_not(low)
        query = jnp.where(mine, pair, jnp.zeros_like(pair))
        score = dot_nt(query, keys[...]) * scaling + bias[...]
        top = jnp.max(score, axis=1, keepdims=True)
        power = jnp.exp(score - top)
        total = jnp.sum(power, axis=1, keepdims=True)
        share = (power * (1.0 / total)).astype(bf16)
        outs.append(dot_nn(share, values[...]))
        logs.append(jnp.broadcast_to(top + jnp.log(total), pair.shape))
    o_ref[...] = jnp.where(low, outs[0], outs[1]).astype(bf16)
    lse_ref[...] = jnp.where(low, logs[0], logs[1])


def attend(q, kvo, kvx, qi, qd, ki, kd):
    rows, width = q.shape
    keys = 2 * kvo.shape[0]
    block = min(256, rows)
    whole = lambda i, j: (0, 0)
    return pl.pallas_call(
        functools.partial(attend_kernel, 1.0 / math.sqrt(HEAD_DIM)),
        grid=(rows // block, width // LANES),
        in_specs=[
            pl.BlockSpec((block, LANES), lambda i, j: (i, j)),
            pl.BlockSpec(kvo.shape, whole),
            pl.BlockSpec(kvx.shape, whole),
            pl.BlockSpec((block, 1), lambda i, j: (i, 0)),
            pl.BlockSpec((block, 1), lambda i, j: (i, 0)),
            pl.BlockSpec((1, keys), whole),
            pl.BlockSpec((1, keys), whole),
        ],
        out_specs=[
            pl.BlockSpec((block, LANES), lambda i, j: (i, j)),
            pl.BlockSpec((block, LANES), lambda i, j: (i, j)),
        ],
        out_shape=(jax.ShapeDtypeStruct(q.shape, bf16), jax.ShapeDtypeStruct(q.shape, f32)),
        scratch_shapes=[
            pltpu.VMEM((keys, LANES), bf16),
            pltpu.VMEM((keys, LANES), bf16),
            pltpu.VMEM((block, keys), f32),
        ],
        compiler_params=pltpu.CompilerParams(vmem_limit_bytes=32 << 20),
        cost_estimate=pl.CostEstimate(
            flops=8 * rows * keys * width, bytes_accessed=rows * width * 8, transcendentals=rows * keys * width // HEAD_DIM
        ),
        name="attend",
    )(q, kvo, kvx, qi, qd, ki, kd)


def attend_back_kernel(
    scaling, q_ref, do_ref, lse_ref, kvo_ref, kvx_ref, qi_ref, qd_ref, ki_ref, kd_ref, cos_ref, sin_ref,
    dq_ref, dkvo_ref, dkvx_ref, keys, values, bias, dk, dv,
):
    first = (pl.program_id(0) == 0) & (pl.program_id(1) == 0)
    last = (pl.program_id(0) == pl.num_programs(0) - 1) & (pl.program_id(1) == pl.num_programs(1) - 1)

    @pl.when(first)
    def _():
        spread_keys(kvo_ref, kvx_ref, keys, values)
        dk[...] = jnp.zeros_like(dk)
        dv[...] = jnp.zeros_like(dv)

    @pl.when(pl.program_id(1) == 0)
    def _():
        bias[...] = mask_bias(qi_ref, qd_ref, ki_ref, kd_ref)

    pair, slope_pair = q_ref[...], do_ref[...]
    low = first_lanes(pair.shape)
    parts = []
    for parity in range(2):
        mine = low if parity == 0 else jnp.logical_not(low)
        query = jnp.where(mine, pair, jnp.zeros_like(pair))
        slope = jnp.where(mine, slope_pair, jnp.zeros_like(slope_pair))
        log_total = lse_ref[:, pl.ds(parity * HEAD_DIM, 1)]
        share = jnp.exp(dot_nt(query, keys[...]) * scaling + bias[...] - log_total)
        dp = dot_nt(slope, values[...])
        delta = jnp.sum(share * dp, axis=1, keepdims=True)
        ds = (share * (dp - delta)).astype(bf16)
        parts.append(dot_nn(ds, keys[...]))
        dk[...] += dot_tn(ds, query)
        dv[...] += dot_tn(share.astype(bf16), slope)
    dq = jnp.where(low, parts[0], parts[1]) * scaling
    dq_ref[...] = rotate(dq, cos_ref[...], -sin_ref[...]).astype(bf16)

    @pl.when(last)
    def _():
        whole_k = (dk[...] + pltpu.roll(dk[...], HEAD_DIM, 1)) * scaling
        whole_v = dv[...] + pltpu.roll(dv[...], HEAD_DIM, 1)
        both = jnp.where(first_lanes(whole_k.shape), whole_k, whole_v)
        rows = dkvo_ref.shape[0]
        dkvo_ref[...] = both[:rows]
        dkvx_ref[...] = both[rows:].astype(bf16)


def attend_back(q, do, lse, kvo, kvx, qi, qd, ki, kd, cosine, sine):
    rows, width = q.shape
    keys = 2 * kvo.shape[0]
    block = min(256, rows)
    whole = lambda i, j: (0, 0)
    tile = pl.BlockSpec((block, LANES), lambda i, j: (i, j))
    row = pl.BlockSpec((block, LANES), lambda i, j: (i, 0))
    column = pl.BlockSpec((block, 1), lambda i, j: (i, 0))
    return pl.pallas_call(
        functools.partial(attend_back_kernel, 1.0 / math.sqrt(HEAD_DIM)),
        grid=(rows // block, width // LANES),
        in_specs=[
            tile, tile, tile,
            pl.BlockSpec(kvo.shape, whole),
            pl.BlockSpec(kvx.shape, whole),
            column, column,
            pl.BlockSpec((1, keys), whole),
            pl.BlockSpec((1, keys), whole),
            row, row,
        ],
        out_specs=[tile, pl.BlockSpec(kvo.shape, whole), pl.BlockSpec(kvx.shape, whole)],
        out_shape=(
            jax.ShapeDtypeStruct(q.shape, bf16),
            jax.ShapeDtypeStruct(kvo.shape, f32),
            jax.ShapeDtypeStruct(kvx.shape, bf16),
        ),
        scratch_shapes=[
            pltpu.VMEM((keys, LANES), bf16),
            pltpu.VMEM((keys, LANES), bf16),
            pltpu.VMEM((block, keys), f32),
            pltpu.VMEM((keys, LANES), f32),
            pltpu.VMEM((keys, LANES), f32),
        ],
        compiler_params=pltpu.CompilerParams(vmem_limit_bytes=40 << 20),
        cost_estimate=pl.CostEstimate(
            flops=20 * rows * keys * width, bytes_accessed=rows * width * 12,
            transcendentals=rows * keys * width // HEAD_DIM,
        ),
        name="attend_back",
    )(q, do, lse, kvo, kvx, qi, qd, ki, kd, cosine, sine)


def ordered(flag, mine, theirs, axis=0):
    return jnp.where(
        flag == 0, jnp.concatenate([mine, theirs], axis=axis), jnp.concatenate([theirs, mine], axis=axis)
    )


def pair_rows(weight, core):
    columns = weight.shape[1] // 2
    mine = lax.dynamic_slice_in_dim(weight, core * columns, columns, axis=1)
    other = lax.dynamic_slice_in_dim(weight, (1 - core) * columns, columns, axis=1)
    return mine, other


def pack_rows(weights, core):
    halves = [pair_rows(weight, core) for weight in weights]
    mine = jnp.concatenate([half[0] for half in halves], axis=1)
    other = jnp.concatenate([half[1] for half in halves], axis=1)
    return ordered(core, mine, lax.ppermute(other, "cc", SWAP))


def unpack_rows(block, core):
    rows = block.shape[0] // 2
    mine = lax.dynamic_slice_in_dim(block, core * rows, rows, axis=0)
    other = lax.dynamic_slice_in_dim(block, (1 - core) * rows, rows, axis=0)
    got = lax.ppermute(other, "cc", SWAP)
    return mine, got


def gather_tokens(own):
    near = lax.ppermute(own, "tp", NEAR)
    far_own = lax.ppermute(own, "cc", SWAP)
    far_near = lax.ppermute(near, "cc", SWAP)
    return jnp.concatenate([own, near, far_own, far_near], axis=0)


def reduce_tokens(make_part, rows):
    theirs = make_part(rows // 2, rows).astype(bf16)
    got = lax.ppermute(theirs, "cc", SWAP)
    own = make_part(0, rows // 2)
    piece = own + got.astype(f32)
    keep = rows // 4
    got_near = lax.ppermute(piece[keep:].astype(bf16), "tp", NEAR)
    here = (piece[:keep] + got_near.astype(f32)).astype(bf16)
    there = lax.ppermute(here, "tp", FAR)
    return here.astype(f32) + there.astype(f32)


def rms_scale(values_in):
    return lax.rsqrt(jnp.mean(values_in * values_in, axis=-1, keepdims=True) + EPSILON)


def norm_back(grad_in, gain_row, normed_in, row_scale):
    scaled = grad_in * gain_row
    return row_scale * (scaled - normed_in * jnp.mean(scaled * normed_in, axis=-1, keepdims=True))


def tp_sum(value):
    value = value + lax.ppermute(value, "tp", NEAR)
    return value + lax.ppermute(value, "tp", FAR)


def shards(
    tokens, doc_ids, positions, attn_gain, q_weight, k_weight, v_weight, o_weight,
    mlp_gain, gate_weight, up_weight, down_weight, out_grad,
):
    layers = q_weight.shape[0]
    piece = tokens.shape[0]
    keep = piece // 2
    rows = 2 * piece
    core = lax.axis_index("cc")
    here = lax.axis_index("cx")
    tp = lax.axis_index("tp")
    half = lax.rem(tp, 2) ^ (tp // 2)
    attn_columns = (q_weight.shape[2], k_weight.shape[2], v_weight.shape[2])
    attn_width = sum(attn_columns) // 2
    hidden_width = gate_weight.shape[2] // 2

    def kept_order(own):
        return ordered(half, own[:keep], own[keep:])

    attn_full, o_full, gu_full, down_full = [], [], [], []
    for layer in range(layers):
        attn_block = pack_rows([q_weight[layer], k_weight[layer], v_weight[layer], o_weight[layer]], core)
        mlp_block = pack_rows([gate_weight[layer], up_weight[layer], down_weight[layer]], core)
        attn_all = lax.all_gather(attn_block, PLANE, axis=0, tiled=True)
        mlp_all = lax.all_gather(mlp_block, PLANE, axis=0, tiled=True)
        attn_full.append(attn_all[:, :attn_width])
        o_full.append(attn_all[:, attn_width:])
        gu_full.append(mlp_all[:, : 2 * hidden_width])
        down_full.append(mlp_all[:, 2 * hidden_width :])
    gains = lax.all_gather(
        jnp.concatenate([attn_gain, mlp_gain], axis=0), ALL_ROWS, axis=1, tiled=True
    ).astype(f32)

    def row_index(place):
        own = here * rows if place == 0 else (1 - here) * rows
        starts = []
        for pair_part in (core, 1 - core):
            for half_part in (half, 1 - half):
                starts.append(own + pair_part * piece + half_part * keep)
        index = jnp.concatenate([start + jnp.arange(keep, dtype=jnp.int32) for start in starts])
        docs = jnp.concatenate([lax.dynamic_slice_in_dim(doc_ids, start, keep) for start in starts])
        return index, docs

    own_index, own_docs = row_index(0)
    other_index, other_docs = row_index(1)
    qi, qd = own_index[:, None], own_docs[:, None]
    ki = jnp.concatenate([own_index, other_index])[None, :]
    kd = jnp.concatenate([own_docs, other_docs])[None, :]

    position_own = kept_order(positions)
    position_all = jnp.concatenate([position_own, lax.ppermute(position_own, "cc", SWAP)])
    lane = jnp.arange(LANES, dtype=jnp.int32)
    inverse = jnp.exp((lane % (HEAD_DIM // 2)).astype(f32) * (-2.0 * math.log(ROPE_BASE) / HEAD_DIM))
    angles = position_all.astype(f32)[:, None] * inverse[None, :]
    cosine = jnp.cos(angles)
    sine = jnp.where((lane % HEAD_DIM < HEAD_DIM // 2)[None, :], -jnp.sin(angles), jnp.sin(angles))

    start = kept_order(tokens).astype(f32)
    x_own = start[:keep]
    kept = []
    for layer in range(layers):
        gain_one = gains[layer][None, :]
        gain_two = gains[layers + layer][None, :]
        if layer == 0:
            own = (start * rms_scale(start) * gain_one).astype(bf16)
            a_all = jnp.concatenate([own, lax.ppermute(own, "cc", SWAP)], axis=0)
            scale_one = rms_scale(x_own)
            n_one = x_own * scale_one
        else:
            scale_one = rms_scale(x_own)
            n_one = x_own * scale_one
            a_all = gather_tokens((n_one * gain_one).astype(bf16))
        queries, kv_own = rope_forward(dot_nn(a_all, attn_full[layer]), cosine, sine)
        kv_other = lax.ppermute(kv_own, "cx", SWAP)
        attended, log_total = attend(queries, kv_own, kv_other, qi, qd, ki, kd)
        x_mid = x_own + reduce_tokens(lambda lo, hi: dot_nt(attended[lo:hi], o_full[layer]), rows)
        scale_two = rms_scale(x_mid)
        n_two = x_mid * scale_two
        b_all = gather_tokens((n_two * gain_two).astype(bf16))
        gate_up = dot_nn(b_all, gu_full[layer])
        gate, up = gate_up[:, :hidden_width], gate_up[:, hidden_width:]
        hidden = (gate * jax.nn.sigmoid(gate) * up).astype(bf16)
        x_own = x_mid + reduce_tokens(lambda lo, hi: dot_nt(hidden[lo:hi], down_full[layer]), rows)
        kept.append(
            (scale_one, n_one, a_all, queries, kv_own, kv_other, log_total, attended, scale_two, n_two, b_all, gate, up, hidden)
        )

    out_own = x_own.astype(bf16)
    output = kept_order(jnp.concatenate([out_own, lax.ppermute(out_own, "tp", NEAR)], axis=0))

    grads = [None] * layers
    slope_own = kept_order(out_grad)
    gm_all = jnp.concatenate([slope_own, lax.ppermute(slope_own, "cc", SWAP)], axis=0)
    g_own = slope_own[:keep].astype(f32)
    for layer in reversed(range(layers)):
        (scale_one, n_one, a_all, queries, kv_own, kv_other, log_total, attended, scale_two, n_two, b_all, gate, up, hidden) = kept[layer]
        gain_one = gains[layer][None, :]
        gain_two = gains[layers + layer][None, :]
        if layer != layers - 1:
            gm_all = gather_tokens(g_own.astype(bf16))
        dh = dot_nn(gm_all, down_full[layer])
        sig = jax.nn.sigmoid(gate)
        dgate = (dh * up * sig * (1.0 + gate * (1.0 - sig))).astype(bf16)
        dup = (dh * (gate * sig)).astype(bf16)
        dgu = jnp.concatenate([dgate, dup], axis=1)
        db = reduce_tokens(lambda lo, hi: dot_nt(dgu[lo:hi], gu_full[layer]), rows)
        mlp_sums = lax.psum_scatter(
            jnp.concatenate(
                [dot_tn(b_all, dgu).astype(bf16), dot_tn(gm_all, hidden).astype(bf16)], axis=1
            ),
            PLANE, scatter_dimension=0, tiled=True,
        )
        g_own = g_own + norm_back(db, gain_two, n_two, scale_two)
        ga_all = gather_tokens(g_own.astype(bf16))
        dob = dot_nn(ga_all, o_full[layer]).astype(bf16)
        dq, dkv_own, dkv_other = attend_back(queries, dob, log_total, kv_own, kv_other, qi, qd, ki, kd, cosine, sine)
        dkv = kv_backward(dkv_own, lax.ppermute(dkv_other, "cx", SWAP), cosine, sine)
        dqkv = jnp.concatenate([dq, dkv], axis=1)
        da = reduce_tokens(lambda lo, hi: dot_nt(dqkv[lo:hi], attn_full[layer]), rows)
        attn_sums = lax.psum_scatter(
            jnp.concatenate(
                [dot_tn(a_all, dqkv).astype(bf16), dot_tn(ga_all, attended).astype(bf16)], axis=1
            ),
            PLANE, scatter_dimension=0, tiled=True,
        )
        g_own = g_own + norm_back(da, gain_one, n_one, scale_one)
        grads[layer] = (unpack_rows(attn_sums, core), unpack_rows(mlp_sums, core))

    last = g_own.astype(bf16)
    tokens_grad = kept_order(jnp.concatenate([last, lax.ppermute(last, "tp", NEAR)], axis=0)).astype(f32)

    def assemble(block, lo, hi):
        return ordered(core, block[0][:, lo:hi].astype(f32), block[1][:, lo:hi].astype(f32), axis=1)

    outs = {name: [] for name in ("q", "k", "v", "o", "gate", "up", "down")}
    gain_parts = []
    for layer in range(layers):
        attn_block, mlp_block = grads[layer]
        at = 0
        for name, columns in zip("qkv", attn_columns):
            outs[name].append(assemble(attn_block, at, at + columns // 2))
            at += columns // 2
        outs["o"].append(assemble(attn_block, at, attn_block[0].shape[1]))
        for number, name in enumerate(("gate", "up", "down")):
            outs[name].append(assemble(mlp_block, number * hidden_width, (number + 1) * hidden_width))

    def row_sum(weight, grad):
        return jnp.sum(weight.astype(f32) * grad, axis=1)

    attn_parts = [
        row_sum(q_weight[layer], outs["q"][layer])
        + row_sum(k_weight[layer], outs["k"][layer])
        + row_sum(v_weight[layer], outs["v"][layer])
        for layer in range(layers)
    ]
    mlp_parts = [
        row_sum(gate_weight[layer], outs["gate"][layer]) + row_sum(up_weight[layer], outs["up"][layer])
        for layer in range(layers)
    ]
    gain_sums = tp_sum(jnp.stack(attn_parts + mlp_parts))
    attn_gain_grad = gain_sums[:layers] / attn_gain.astype(f32)
    mlp_gain_grad = gain_sums[layers:] / mlp_gain.astype(f32)

    stacked = {name: jnp.stack(parts) for name, parts in outs.items()}
    return (
        output, tokens_grad, attn_gain_grad, stacked["q"], stacked["k"], stacked["v"], stacked["o"],
        mlp_gain_grad, stacked["gate"], stacked["up"], stacked["down"],
    )


def solution(mesh):
    fsdp, ctx, tp = (mesh.shape[name] for name in ("fsdp", "ctx", "tp"))
    assert ctx == 4 and tp == 4
    split = Mesh(mesh.devices.reshape(fsdp, ctx // 2, 2, tp), ("fsdp", "cx", "cc", "tp"))
    row = P(ALL_ROWS, None)
    gain = P(None, ALL_ROWS)
    weight = P(None, ALL_ROWS, "tp")
    in_specs = (
        row, P("fsdp"), P(ALL_ROWS), gain, weight, weight, weight, weight, gain, weight, weight, weight, row,
    )
    out_specs = (row, row, gain, weight, weight, weight, weight, gain, weight, weight, weight)
    return jax.shard_map(shards, mesh=split, in_specs=in_specs, out_specs=out_specs, check_vma=False)
```

```python
import functools
import math

import jax
import jax.numpy as jnp
from jax import lax
from jax.experimental import pallas as pl
from jax.experimental.pallas import tpu as pltpu
from jax.sharding import Mesh
from jax.sharding import PartitionSpec as P

HEAD_DIM = 64
LANES = 128
ROPE_BASE = 500000.0
EPSILON = 1e-05
NEGATIVE = -1e30


PLANE = ("fsdp", "cx")
ALL_ROWS = ("fsdp", "cx", "cc")
NEAR = [(0, 1), (1, 0), (2, 3), (3, 2)]
FAR = [(0, 3), (3, 0), (1, 2), (2, 1)]
SWAP = [(0, 1), (1, 0)]

f32 = jnp.float32
bf16 = jnp.bfloat16


def dot_nn(a, b):
    return lax.dot_general(a, b, (((1,), (0,)), ((), ())), preferred_element_type=f32)


def dot_nt(a, b):
    return lax.dot_general(a, b, (((1,), (1,)), ((), ())), preferred_element_type=f32)


def dot_tn(a, b):
    return lax.dot_general(a, b, (((0,), (0,)), ((), ())), preferred_element_type=f32)


def swap_halves(slab):
    lane = lax.broadcasted_iota(jnp.int32, slab.shape, 1)
    low = lax.rem(lane, HEAD_DIM) < HEAD_DIM // 2
    return jnp.where(low, pltpu.roll(slab, LANES - HEAD_DIM // 2, 1), pltpu.roll(slab, HEAD_DIM // 2, 1))


def rotate(slab, cosine, sine):
    return slab * cosine + swap_halves(slab) * sine


def first_lanes(shape):
    return lax.broadcasted_iota(jnp.int32, shape, 1) < HEAD_DIM


def rope_kernel(x_ref, cos_ref, sin_ref, q_ref, kv_ref):
    cosine, sine = cos_ref[...], sin_ref[...]
    slabs = q_ref.shape[1] // LANES
    for j in range(slabs):
        part = pl.ds(j * LANES, LANES)
        q_ref[:, part] = rotate(x_ref[:, part], cosine, sine).astype(bf16)
    kv = x_ref[:, pl.ds(slabs * LANES, LANES)]
    kv_ref[...] = jnp.where(first_lanes(kv.shape), rotate(kv, cosine, sine), kv).astype(bf16)


def rope_forward(x, cosine, sine):
    rows, width = x.shape
    return pl.pallas_call(
        rope_kernel,
        out_shape=(
            jax.ShapeDtypeStruct((rows, width - LANES), bf16),
            jax.ShapeDtypeStruct((rows, LANES), bf16),
        ),
        cost_estimate=pl.CostEstimate(flops=rows * width * 6, bytes_accessed=rows * width * 8, transcendentals=0),
        name="rope_forward",
    )(x, cosine, sine)


def kv_back_kernel(own_ref, got_ref, cos_ref, sin_ref, out_ref):
    total = own_ref[...] + got_ref[...].astype(f32)
    out_ref[...] = jnp.where(
        first_lanes(total.shape), rotate(total, cos_ref[...], -sin_ref[...]), total
    ).astype(bf16)


def kv_backward(own, got, cosine, sine):
    return pl.pallas_call(
        kv_back_kernel,
        out_shape=jax.ShapeDtypeStruct(own.shape, bf16),
        cost_estimate=pl.CostEstimate(flops=own.size * 6, bytes_accessed=own.size * 16, transcendentals=0),
        name="kv_backward",
    )(own, got, cosine, sine)


def spread_keys(kv_refs, keys, values):
    at = 0
    for ref in kv_refs:
        both = ref[...].astype(f32)
        turned = pltpu.roll(both, HEAD_DIM, 1)
        low = first_lanes(both.shape)
        part = pl.ds(at, ref.shape[0])
        keys[part, :] = jnp.where(low, both, turned).astype(bf16)
        values[part, :] = jnp.where(low, turned, both).astype(bf16)
        at += ref.shape[0]


def mask_bias(qi_ref, qd_ref, ki_ref, kd_ref):
    seen = (ki_ref[...] <= qi_ref[...]) & (kd_ref[...] == qd_ref[...])
    return jnp.where(seen, 0.0, NEGATIVE)


def attend_kernel(scaling, pieces, q_ref, *refs):
    kv_refs = refs[:pieces]
    qi_ref, qd_ref, ki_ref, kd_ref, o_ref, lse_ref, keys, values, bias = refs[pieces:]

    @pl.when(pl.program_id(0) == 0)
    def _():
        spread_keys(kv_refs, keys, values)
        bias[...] = mask_bias(qi_ref, qd_ref, ki_ref, kd_ref)

    pair = q_ref[...]
    low = first_lanes(pair.shape)
    outs, logs = [], []
    for parity in range(2):
        mine = low if parity == 0 else jnp.logical_not(low)
        query = jnp.where(mine, pair, jnp.zeros_like(pair))
        score = dot_nt(query, keys[...]) * scaling + bias[...]
        top = jnp.max(score, axis=1, keepdims=True)
        power = jnp.exp(score - top)
        total = jnp.sum(power, axis=1, keepdims=True)
        share = (power * (1.0 / total)).astype(bf16)
        outs.append(dot_nn(share, values[...]))
        logs.append(jnp.broadcast_to(top + jnp.log(total), pair.shape))
    o_ref[...] = jnp.where(low, outs[0], outs[1]).astype(bf16)
    lse_ref[...] = jnp.where(low, logs[0], logs[1])


def attend(q, kv_pieces, qi, qd, ki, kd):
    rows, width = q.shape
    keys = ki.shape[1]
    whole = lambda j: (0, 0)
    slab = pl.BlockSpec((rows, LANES), lambda j: (0, j))
    full = lambda x: pl.BlockSpec(x.shape, whole)
    return pl.pallas_call(
        functools.partial(attend_kernel, 1.0 / math.sqrt(HEAD_DIM), len(kv_pieces)),
        grid=(width // LANES,),
        in_specs=[slab] + [full(x) for x in (*kv_pieces, qi, qd, ki, kd)],
        out_specs=[slab, slab],
        out_shape=(jax.ShapeDtypeStruct(q.shape, bf16), jax.ShapeDtypeStruct(q.shape, f32)),
        scratch_shapes=[
            pltpu.VMEM((keys, LANES), bf16),
            pltpu.VMEM((keys, LANES), bf16),
            pltpu.VMEM((rows, keys), f32),
        ],
        compiler_params=pltpu.CompilerParams(vmem_limit_bytes=24 << 20),
        cost_estimate=pl.CostEstimate(
            flops=8 * rows * keys * width, bytes_accessed=rows * width * 8, transcendentals=rows * keys * width // HEAD_DIM
        ),
        name="attend",
    )(q, *kv_pieces, qi, qd, ki, kd)


def attend_back_kernel(scaling, pieces, carried, finish, q_ref, do_ref, lse_ref, *refs):
    kv_refs, refs = refs[:pieces], refs[pieces:]
    qi_ref, qd_ref, ki_ref, kd_ref, cos_ref, sin_ref = refs[:6]
    refs = refs[6:]
    if carried:
        dk_in, dv_in, refs = refs[0], refs[1], refs[2:]
    if finish:
        dq_ref, own_ref, other_ref, keys, values, bias, dk, dv = refs
    else:
        dq_ref, dk, dv, keys, values, bias = refs

    @pl.when(pl.program_id(0) == 0)
    def _():
        spread_keys(kv_refs, keys, values)
        bias[...] = mask_bias(qi_ref, qd_ref, ki_ref, kd_ref)
        dk[...] = dk_in[...] if carried else jnp.zeros_like(dk)
        dv[...] = dv_in[...] if carried else jnp.zeros_like(dv)

    pair, slope_pair = q_ref[...], do_ref[...]
    low = first_lanes(pair.shape)
    parts = []
    for parity in range(2):
        mine = low if parity == 0 else jnp.logical_not(low)
        query = jnp.where(mine, pair, jnp.zeros_like(pair))
        slope = jnp.where(mine, slope_pair, jnp.zeros_like(slope_pair))
        log_total = lse_ref[:, pl.ds(parity * HEAD_DIM, 1)]
        share = jnp.exp(dot_nt(query, keys[...]) * scaling + bias[...] - log_total)
        dp = dot_nt(slope, values[...])
        delta = jnp.sum(share * dp, axis=1, keepdims=True)
        ds = (share * (dp - delta)).astype(bf16)
        parts.append(dot_nn(ds, keys[...]))
        dk[...] += dot_tn(ds, query)
        dv[...] += dot_tn(share.astype(bf16), slope)
    dq = jnp.where(low, parts[0], parts[1]) * scaling
    dq_ref[...] = rotate(dq, cos_ref[...], -sin_ref[...]).astype(bf16)

    if finish:

        @pl.when(pl.program_id(0) == pl.num_programs(0) - 1)
        def _():
            whole_k = (dk[...] + pltpu.roll(dk[...], HEAD_DIM, 1)) * scaling
            whole_v = dv[...] + pltpu.roll(dv[...], HEAD_DIM, 1)
            both = jnp.where(first_lanes(whole_k.shape), whole_k, whole_v)
            rows = own_ref.shape[0]
            own_ref[...] = both[:rows]
            other_ref[...] = both[rows:].astype(bf16)


def attend_back(q, do, lse, kv_pieces, qi, qd, ki, kd, cosine, sine, sums, finish):
    rows, width = q.shape
    keys = ki.shape[1]
    whole = lambda j: (0, 0)
    slab = pl.BlockSpec((rows, LANES), lambda j: (0, j))
    full = lambda x: pl.BlockSpec(x.shape, whole)
    carried = sums is not None
    operands = (*kv_pieces, qi, qd, ki, kd, cosine, sine, *(sums if carried else ()))
    sum_spec = pl.BlockSpec((keys, LANES), whole)
    sum_shape = jax.ShapeDtypeStruct((keys, LANES), f32)
    work = [
        pltpu.VMEM((keys, LANES), bf16),
        pltpu.VMEM((keys, LANES), bf16),
        pltpu.VMEM((rows, keys), f32),
    ]
    half_spec = pl.BlockSpec((keys // 2, LANES), whole)
    if finish:
        out_specs = [slab, half_spec, half_spec]
        out_shape = (
            jax.ShapeDtypeStruct(q.shape, bf16),
            jax.ShapeDtypeStruct((keys // 2, LANES), f32),
            jax.ShapeDtypeStruct((keys // 2, LANES), bf16),
        )
        work = work + [pltpu.VMEM((keys, LANES), f32), pltpu.VMEM((keys, LANES), f32)]
    else:
        out_specs = [slab, sum_spec, sum_spec]
        out_shape = (jax.ShapeDtypeStruct(q.shape, bf16), sum_shape, sum_shape)
    return pl.pallas_call(
        functools.partial(attend_back_kernel, 1.0 / math.sqrt(HEAD_DIM), len(kv_pieces), carried, finish),
        grid=(width // LANES,),
        in_specs=[slab, slab, slab] + [full(x) for x in operands],
        out_specs=out_specs,
        out_shape=out_shape,
        scratch_shapes=work,
        compiler_params=pltpu.CompilerParams(vmem_limit_bytes=32 << 20),
        cost_estimate=pl.CostEstimate(
            flops=20 * rows * keys * width, bytes_accessed=rows * width * 12,
            transcendentals=rows * keys * width // HEAD_DIM,
        ),
        name="attend_back",
    )(q, do, lse, *operands)


def grad_kernel(chunks, *refs):
    out_ref = refs[-1]
    at = 0
    for side in range(2):
        lefts = refs[2 * side * chunks : (2 * side + 1) * chunks]
        rights = refs[(2 * side + 1) * chunks : (2 * side + 2) * chunks]
        width = rights[0].shape[1]
        total = dot_tn(lefts[0][...], rights[0][...])
        for left, right in zip(lefts[1:], rights[1:]):
            total += dot_tn(left[...], right[...])
        out_ref[:, pl.ds(at, width)] = total.astype(bf16)
        at += width


def weight_grads(left_a, right_a, left_b, right_b):
    chunks = len(left_a)
    rows, depth = left_a[0].shape
    width = right_a[0].shape[1] + right_b[0].shape[1]
    block = min(256, depth)
    left = pl.BlockSpec((rows, block), lambda i: (0, i))
    whole = lambda x: pl.BlockSpec(x.shape, lambda i: (0, 0))
    operands = (*left_a, *right_a, *left_b, *right_b)
    specs = [left] * chunks + [whole(x) for x in right_a] + [left] * chunks + [whole(x) for x in right_b]
    return pl.pallas_call(
        functools.partial(grad_kernel, chunks),
        grid=(depth // block,),
        in_specs=specs,
        out_specs=pl.BlockSpec((block, width), lambda i: (i, 0)),
        out_shape=jax.ShapeDtypeStruct((depth, width), bf16),
        compiler_params=pltpu.CompilerParams(vmem_limit_bytes=40 << 20),
        cost_estimate=pl.CostEstimate(
            flops=2 * chunks * rows * depth * width, bytes_accessed=2 * depth * width + 4 * rows * depth * chunks,
            transcendentals=0,
        ),
        name="weight_grads",
    )(*operands)


def place_kernel(counts, core_ref, mine_ref, got_ref, *refs):
    arrays = len(counts)
    weights = refs[:arrays]
    outs = refs[len(refs) - arrays - 1 : len(refs) - 1]
    sum_ref = refs[-1]
    second = core_ref[0] == 1
    at = 0
    total = None
    for width, weighted, weight_ref, out_ref in zip(*zip(*counts), weights, outs):
        part = pl.ds(at, width)
        mine, got = mine_ref[:, part].astype(f32), got_ref[:, part].astype(f32)
        if width % LANES == 0:
            out_ref[0, :, pl.ds(0, width)] = jnp.where(second, got, mine)
            out_ref[0, :, pl.ds(width, width)] = jnp.where(second, mine, got)
        else:
            pair = jnp.concatenate([mine, got], axis=1)
            out_ref[0, :, :] = jnp.where(second, pltpu.roll(pair, width, 1), pair)
        if weighted:
            row = jnp.sum(weight_ref[0].astype(f32) * out_ref[0], axis=1, keepdims=True)
            total = row if total is None else total + row
        at += width
    sum_ref[...] = jnp.broadcast_to(total, sum_ref.shape)


def place_grads(core, block, got, weights, weighted, layer, layers, before):
    rows = got.shape[0]
    widths = [w.shape[2] // 2 for w in weights]
    step = min(64, rows)
    steps = rows // step
    stacked = [jax.ShapeDtypeStruct((layers, rows, 2 * width), f32) for width in widths]
    slab = [pl.BlockSpec((1, step, 2 * width), lambda i, c: (layer, i, 0)) for width in widths]
    wide = block.shape[1]
    specs = [
        pl.BlockSpec((step, wide), lambda i, c: (c[0] * steps + i, 0)),
        pl.BlockSpec((step, wide), lambda i, c: (i, 0)),
    ] + slab
    operands = [block, got, *weights]
    aliases = {}
    if before is not None:
        specs += [pl.BlockSpec(memory_space=pl.ANY)] * len(before)
        aliases = {1 + len(operands) + n: n for n in range(len(before))}
        operands += before
    return pl.pallas_call(
        functools.partial(place_kernel, list(zip(widths, weighted))),
        grid_spec=pltpu.PrefetchScalarGridSpec(
            num_scalar_prefetch=1,
            grid=(steps,),
            in_specs=specs,
            out_specs=slab + [pl.BlockSpec((step, LANES), lambda i, c: (i, 0))],
        ),
        out_shape=(*stacked, jax.ShapeDtypeStruct((rows, LANES), f32)),
        input_output_aliases=aliases,
        compiler_params=pltpu.CompilerParams(vmem_limit_bytes=32 << 20),
        cost_estimate=pl.CostEstimate(flops=4 * rows * wide, bytes_accessed=rows * wide * 16, transcendentals=0),
        name="place_grads",
    )(core.reshape(1), *operands)


def pack_kernel(widths, core_ref, *refs):
    got_ref, out_ref = refs[-2], refs[-1]
    own = pl.program_id(0) == core_ref[0]

    @pl.when(own)
    def _():
        at = 0
        for width, ref in zip(widths, refs):
            out_ref[:, pl.ds(at, width)] = ref[0]
            at += width

    @pl.when(jnp.logical_not(own))
    def _():
        out_ref[...] = got_ref[...]


def pick_kernel(widths, core_ref, *refs):
    out_ref = refs[-1]
    at = 0
    for width, ref in zip(widths, refs):
        out_ref[:, pl.ds(at, width)] = ref[0]
        at += width


def pack_wide(weights, layer, core):
    rows = weights[0].shape[1]
    widths = [w.shape[2] // 2 for w in weights]
    wide = sum(widths)
    core = core.reshape(1)
    cost = pl.CostEstimate(flops=0, bytes_accessed=4 * rows * wide, transcendentals=0)
    other = pl.pallas_call(
        functools.partial(pick_kernel, widths),
        grid_spec=pltpu.PrefetchScalarGridSpec(
            num_scalar_prefetch=1,
            grid=(1,),
            in_specs=[pl.BlockSpec((1, rows, width), lambda i, c: (layer, 0, 1 - c[0])) for width in widths],
            out_specs=pl.BlockSpec((rows, wide), lambda i, c: (0, 0)),
        ),
        out_shape=jax.ShapeDtypeStruct((rows, wide), bf16),
        compiler_params=pltpu.CompilerParams(vmem_limit_bytes=24 << 20),
        cost_estimate=cost,
        name="pick_half",
    )(core, *weights)
    got = lax.ppermute(other, "cc", SWAP)
    return pl.pallas_call(
        functools.partial(pack_kernel, widths),
        grid_spec=pltpu.PrefetchScalarGridSpec(
            num_scalar_prefetch=1,
            grid=(2,),
            in_specs=[pl.BlockSpec((1, rows, width), lambda i, c: (layer, 0, c[0])) for width in widths]
            + [pl.BlockSpec((rows, wide), lambda i, c: (0, 0))],
            out_specs=pl.BlockSpec((rows, wide), lambda i, c: (i, 0)),
        ),
        out_shape=jax.ShapeDtypeStruct((2 * rows, wide), bf16),
        compiler_params=pltpu.CompilerParams(vmem_limit_bytes=24 << 20),
        cost_estimate=cost,
        name="pack_half",
    )(core, *weights, got)


CHUNKS = 2


def ordered(flag, mine, theirs, axis=0):
    return jnp.where(
        flag == 0, jnp.concatenate([mine, theirs], axis=axis), jnp.concatenate([theirs, mine], axis=axis)
    )


def pack_rows(weights, core):
    def half(which):
        return jnp.concatenate(
            [
                lax.dynamic_slice_in_dim(w, which * (w.shape[1] // 2), w.shape[1] // 2, axis=1)
                for w in weights
            ],
            axis=1,
        )

    mine = half(core)
    got = lax.ppermute(half(1 - core), "cc", SWAP)
    rows = mine.shape[0]
    block = jnp.zeros((2 * rows, mine.shape[1]), mine.dtype)
    block = lax.dynamic_update_slice_in_dim(block, mine, core * rows, axis=0)
    return lax.dynamic_update_slice_in_dim(block, got, (1 - core) * rows, axis=0)


def plane_gather(block, sizes, place):
    fsdp, cx = sizes
    if fsdp != 2 or cx != 2:
        return lax.all_gather(block, PLANE, axis=0, tiled=True)
    rows = block.shape[0]
    half = rows // 2
    beside = lax.ppermute(block, "cx", SWAP)
    across = lax.ppermute(block, "fsdp", SWAP)
    corner_a = lax.ppermute(beside[:half], "fsdp", SWAP)
    corner_b = lax.ppermute(across[half:], "cx", SWAP)
    f, c = place
    full = jnp.zeros((4 * rows, block.shape[1]), block.dtype)
    for part, at in (
        (block, (2 * f + c) * rows),
        (beside, (2 * f + 1 - c) * rows),
        (across, (2 * (1 - f) + c) * rows),
        (corner_a, (2 * (1 - f) + 1 - c) * rows),
        (corner_b, (2 * (1 - f) + 1 - c) * rows + half),
    ):
        full = lax.dynamic_update_slice_in_dim(full, part, at, axis=0)
    return full


def plane_scatter(full, sizes, place):
    fsdp, cx = sizes
    if fsdp != 2 or cx != 2:
        return lax.psum_scatter(full, PLANE, scatter_dimension=0, tiled=True)
    rows = full.shape[0] // 4
    half = rows // 2
    f, c = place
    take = lambda at, count: lax.dynamic_slice_in_dim(full, at, count, axis=0)
    beside_at = (2 * f + 1 - c) * rows
    across_at = (2 * (1 - f) + c) * rows
    corner_at = (2 * (1 - f) + 1 - c) * rows
    corner_a = lax.ppermute(take(corner_at, half), "cx", SWAP)
    corner_b = lax.ppermute(take(corner_at + half, half), "fsdp", SWAP)
    beside_a = lax.ppermute(take(beside_at, half), "cx", SWAP)
    across_b = lax.ppermute(take(across_at + half, half), "fsdp", SWAP)
    add = lambda x, y: (x.astype(f32) + y.astype(f32)).astype(bf16)
    across_a = lax.ppermute(add(take(across_at, half), corner_a), "fsdp", SWAP)
    beside_b = lax.ppermute(add(take(beside_at + half, half), corner_b), "cx", SWAP)
    own_at = (2 * f + c) * rows
    own = take(own_at, rows).astype(f32)
    return jnp.concatenate(
        [
            own[:half] + beside_a.astype(f32) + across_a.astype(f32),
            own[half:] + beside_b.astype(f32) + across_b.astype(f32),
        ]
    ).astype(bf16)


def gather_tokens(own):
    near = lax.ppermute(own, "tp", NEAR)
    pair_own = lax.ppermute(own, "cc", SWAP)
    pair_near = lax.ppermute(near, "cc", SWAP)
    return jnp.concatenate([own, near, pair_own, pair_near], axis=0)


def near_sum(part):
    part = part.astype(bf16)
    half = part.shape[0] // 2
    got = lax.ppermute(part[half:], "cc", SWAP)
    piece = part[:half].astype(f32) + got.astype(f32)
    keep = half // 2
    got_near = lax.ppermute(piece[keep:].astype(bf16), "tp", NEAR)
    return (piece[:keep] + got_near.astype(f32)).astype(bf16)


def far_sum(here):
    return here.astype(f32) + lax.ppermute(here, "tp", FAR).astype(f32)


def rms_scale(values_in):
    return lax.rsqrt(jnp.mean(values_in * values_in, axis=-1, keepdims=True) + EPSILON)


def norm_back(grad_in, gain_row, normed_in, row_scale):
    scaled = grad_in * gain_row
    return row_scale * (scaled - normed_in * jnp.mean(scaled * normed_in, axis=-1, keepdims=True))


def tp_sum(value):
    value = value + lax.ppermute(value, "tp", NEAR)
    return value + lax.ppermute(value, "tp", FAR)


def shards(
    tokens, doc_ids, positions, attn_gain, q_weight, k_weight, v_weight, o_weight,
    mlp_gain, gate_weight, up_weight, down_weight, out_grad,
):
    layers = q_weight.shape[0]
    sizes = (lax.axis_size("fsdp"), lax.axis_size("cx"))
    place = (lax.axis_index("fsdp"), lax.axis_index("cx"))
    piece = tokens.shape[0]
    keep = piece // 2
    sub = keep // CHUNKS
    rows = 2 * piece
    core = lax.axis_index("cc")
    here = lax.axis_index("cx")
    tp = lax.axis_index("tp")
    half = lax.rem(tp, 2) ^ (tp // 2)
    attn_width = (q_weight.shape[2] + k_weight.shape[2] + v_weight.shape[2]) // 2
    query_width = q_weight.shape[2] // 2
    hidden_width = gate_weight.shape[2] // 2
    mlp_weights = (gate_weight, up_weight, down_weight)
    chunks = range(CHUNKS)

    def kept_order(own):
        return ordered(half, own[:keep], own[keep:])

    def chunk_of(kept_first, c):
        return jnp.concatenate([kept_first[c * sub : (c + 1) * sub], kept_first[keep + c * sub : keep + (c + 1) * sub]])

    attn_blocks = [
        pack_rows([q_weight[layer], k_weight[layer], v_weight[layer], o_weight[layer]], core)
        for layer in range(layers)
    ]
    attn_all = [plane_gather(block, sizes, place) for block in attn_blocks]
    attn_full = [full[:, :attn_width] for full in attn_all]
    o_full = [full[:, attn_width:] for full in attn_all]
    mlp_all = [
        lax.all_gather(pack_wide(mlp_weights, layer, core), PLANE, axis=0, tiled=True) for layer in range(layers)
    ]
    gu_full = [full[:, : 2 * hidden_width] for full in mlp_all]
    down_full = [full[:, 2 * hidden_width :] for full in mlp_all]
    gains = lax.all_gather(
        jnp.concatenate([attn_gain, mlp_gain], axis=0), ALL_ROWS, axis=1, tiled=True
    ).astype(f32)

    def chunk_index(c, place_x):
        starts = [
            place_x * rows + pair_part * piece + half_part * keep + c * sub
            for pair_part in (core, 1 - core)
            for half_part in (half, 1 - half)
        ]
        index = jnp.concatenate([start + jnp.arange(sub, dtype=jnp.int32) for start in starts])
        docs = jnp.concatenate([lax.dynamic_slice_in_dim(doc_ids, start, sub) for start in starts])
        return index, docs

    own_places = [chunk_index(c, here) for c in chunks]
    other_places = [chunk_index(c, 1 - here) for c in chunks]
    qi = [index[:, None] for index, _ in own_places]
    qd = [docs[:, None] for _, docs in own_places]
    ki = jnp.concatenate([index for index, _ in own_places + other_places])[None, :]
    kd = jnp.concatenate([docs for _, docs in own_places + other_places])[None, :]

    position_own = kept_order(positions)
    position_pair = lax.ppermute(position_own, "cc", SWAP)
    lane = jnp.arange(LANES, dtype=jnp.int32)
    inverse = jnp.exp((lane % (HEAD_DIM // 2)).astype(f32) * (-2.0 * math.log(ROPE_BASE) / HEAD_DIM))
    cosine, sine = [], []
    for c in chunks:
        at = jnp.concatenate([chunk_of(position_own, c), chunk_of(position_pair, c)])
        angles = at.astype(f32)[:, None] * inverse[None, :]
        cosine.append(jnp.cos(angles))
        sine.append(jnp.sin(angles) * jnp.where(lane % HEAD_DIM < HEAD_DIM // 2, -1.0, 1.0)[None, :])

    start = kept_order(tokens)
    start_pair = lax.ppermute(start, "cc", SWAP)
    x_own = [start[c * sub : (c + 1) * sub].astype(f32) for c in chunks]
    kept = []
    for layer in range(layers):
        gain_one = gains[layer][None, :]
        gain_two = gains[layers + layer][None, :]
        scale_one = [rms_scale(x) for x in x_own]
        n_one = [x * s for x, s in zip(x_own, scale_one)]
        a_all, queries, kv_own = [], [], []
        for c in chunks:
            if layer == 0:
                first = jnp.concatenate([chunk_of(start, c), chunk_of(start_pair, c)]).astype(f32)
                a_all.append((first * rms_scale(first) * gain_one).astype(bf16))
            else:
                a_all.append(gather_tokens((n_one[c] * gain_one).astype(bf16)))
            q, kv = rope_forward(dot_nn(a_all[c], attn_full[layer]), cosine[c], sine[c])
            queries.append(q)
            kv_own.append(kv)
        kv_pieces = kv_own + [lax.ppermute(kv, "cx", SWAP) for kv in kv_own]
        attended, log_total, x_mid = [], [], []
        for c in chunks:
            out, log = attend(queries[c], kv_pieces, qi[c], qd[c], ki, kd)
            attended.append(out)
            log_total.append(log)
            x_mid.append(x_own[c] + far_sum(near_sum(dot_nt(out, o_full[layer]))))
        scale_two = [rms_scale(x) for x in x_mid]
        n_two = [x * s for x, s in zip(x_mid, scale_two)]
        b_all, gate_up, hidden = [], [], []
        for c in chunks:
            b_all.append(gather_tokens((n_two[c] * gain_two).astype(bf16)))
            both = dot_nn(b_all[c], gu_full[layer])
            gate, up = both[:, :hidden_width], both[:, hidden_width:]
            hidden.append((gate * jax.nn.sigmoid(gate) * up).astype(bf16))
            gate_up.append((gate, up))
        x_own = [
            x_mid[c] + far_sum(near_sum(dot_nt(hidden[c], down_full[layer]))) for c in chunks
        ]
        kept.append(
            (scale_one, n_one, a_all, queries, kv_pieces, log_total, attended, scale_two, n_two, b_all, gate_up, hidden)
        )

    out_own = jnp.concatenate(x_own).astype(bf16)
    output = kept_order(jnp.concatenate([out_own, lax.ppermute(out_own, "tp", NEAR)], axis=0))

    outs_attn, outs_mlp = None, None
    attn_sums, mlp_sums = [None] * layers, [None] * layers
    slope = kept_order(out_grad)
    slope_pair = lax.ppermute(slope, "cc", SWAP)
    g_own = [slope[c * sub : (c + 1) * sub].astype(f32) for c in chunks]
    for layer in reversed(range(layers)):
        (scale_one, n_one, a_all, queries, kv_pieces, log_total, attended, scale_two, n_two, b_all, gate_up, hidden) = kept[layer]
        gain_one = gains[layer][None, :]
        gain_two = gains[layers + layer][None, :]
        if layer == layers - 1:
            gm_all = [jnp.concatenate([chunk_of(slope, c), chunk_of(slope_pair, c)]) for c in chunks]
        else:
            gm_all = [gather_tokens(g.astype(bf16)) for g in g_own]
        dgu, here_sums = [], []
        for c in chunks:
            dh = dot_nn(gm_all[c], down_full[layer])
            gate, up = gate_up[c]
            sig = jax.nn.sigmoid(gate)
            dgate = (dh * up * sig * (1.0 + gate * (1.0 - sig))).astype(bf16)
            dup = (dh * (gate * sig)).astype(bf16)
            dgu.append(jnp.concatenate([dgate, dup], axis=1))
            here_sums.append(near_sum(dot_nt(dgu[c], gu_full[layer])))
        mlp_part = weight_grads(b_all, dgu, gm_all, hidden)
        here_sums[-1], mlp_part = lax.optimization_barrier((here_sums[-1], mlp_part))
        mlp_got = lax.psum_scatter(mlp_part, PLANE, scatter_dimension=0, tiled=True)
        ga_all, back = [], []
        sums = None
        for c in chunks:
            g_own[c] = g_own[c] + norm_back(far_sum(here_sums[c]), gain_two, n_two[c], scale_two[c])
            ga_all.append(gather_tokens(g_own[c].astype(bf16)))
            dob = dot_nn(ga_all[c], o_full[layer]).astype(bf16)
            dq, *sums = attend_back(
                queries[c], dob, log_total[c], kv_pieces, qi[c], qd[c], ki, kd, cosine[c], sine[c], sums, c == CHUNKS - 1
            )
            back.append(dq)
        dkv_own, dkv_other = sums
        dkv = kv_backward(
            dkv_own, lax.ppermute(dkv_other, "cx", SWAP), jnp.concatenate(cosine), jnp.concatenate(sine)
        )
        dqkv = [
            jnp.concatenate([back[c], dkv[c * 4 * sub : (c + 1) * 4 * sub]], axis=1) for c in chunks
        ]
        here_sums = [near_sum(dot_nt(dqkv[c], attn_full[layer])) for c in chunks]
        attn_part = weight_grads(a_all, dqkv, ga_all, attended)
        here_sums[-1], attn_part = lax.optimization_barrier((here_sums[-1], attn_part))
        attn_got = plane_scatter(attn_part, sizes, place)
        for c in chunks:
            g_own[c] = g_own[c] + norm_back(far_sum(here_sums[c]), gain_one, n_one[c], scale_one[c])

        def pair_half(block):
            count = block.shape[0] // 2
            return lax.ppermute(lax.dynamic_slice_in_dim(block, (1 - core) * count, count, axis=0), "cc", SWAP)

        *outs_attn, attn_sums[layer] = place_grads(
            core, attn_got, pair_half(attn_got), (q_weight, k_weight, v_weight, o_weight),
            (True, True, True, False), layer, layers, outs_attn,
        )
        *outs_mlp, mlp_sums[layer] = place_grads(
            core, mlp_got, pair_half(mlp_got), mlp_weights, (True, True, False), layer, layers, outs_mlp
        )

    last = jnp.concatenate(g_own).astype(bf16)
    tokens_grad = kept_order(jnp.concatenate([last, lax.ppermute(last, "tp", NEAR)], axis=0)).astype(f32)

    def gain_grads(sums, gain):
        return tp_sum(jnp.stack([s[:, 0] for s in sums])) / gain.astype(f32)

    return (
        output, tokens_grad, gain_grads(attn_sums, attn_gain), *outs_attn,
        gain_grads(mlp_sums, mlp_gain), *outs_mlp,
    )


def solution(mesh):
    fsdp, ctx, tp = (mesh.shape[name] for name in ("fsdp", "ctx", "tp"))
    assert ctx == 4 and tp == 4
    split = Mesh(mesh.devices.reshape(fsdp, ctx // 2, 2, tp), ("fsdp", "cx", "cc", "tp"))
    row = P(ALL_ROWS, None)
    gain = P(None, ALL_ROWS)
    weight = P(None, ALL_ROWS, "tp")
    in_specs = (
        row, P("fsdp"), P(ALL_ROWS), gain, weight, weight, weight, weight, gain, weight, weight, weight, row,
    )
    out_specs = (row, row, gain, weight, weight, weight, weight, gain, weight, weight, weight)
    return jax.shard_map(shards, mesh=split, in_specs=in_specs, out_specs=out_specs, check_vma=False)
```
